32 devices in a mesh: segment: 2 (over core), clip: 4 (over z), tile: 4 (over y, x).
Axes of the slice: x: 2, y: 2, z: 4, core: 2. Of those that a mesh axis runs over, the one named last changes fastest.
Arguments:
- video: bfloat16 [4, 4, 3, 12, 4, 256], P('clip', 'tile'), may hold values from -6 to 6
- cotangent: bfloat16 [4, 4, 3, 12, 4, 256], P('clip', 'tile'), may hold values from -6 to 6
- weights: bfloat16 [2, 27, 256, 256], P('segment'), may hold values from -0.078125 to 0.078125
- neighbours: int32 [4, 4, 2], P('clip', 'tile'), may hold values from 0 to 4, as said below
- rows_used: int32 [4, 4], P('clip', 'tile'), may hold values from 3 to 12, as said below
- cols_used: int32 [4], P('clip'), may hold values from 2 to 4, as said below
Outputs:
- section_out: bfloat16 [2, 4, 4, 3, 12, 4, 256], P('segment', 'clip', 'tile')
- grads: float32 [2, 3, 589824], P('segment', None, ('clip', 'tile'))
The draws below stay inside these ranges and needn't reach their ends.
Inputs may be any that keep to these rules, and one draw needn't show every extreme that they name: `neighbours`: in each clip the strips of its frames lie on the 4 tiles in an order of their own: entry 0 names the tile of the strip above, entry 1 the tile of the strip below, 4 where there is none; exactly one strip of each clip has none above and one has none below, and the entries chain all 4 strips of a clip top to bottom. `rows_used`: in every clip some strip has 12 rows. `cols_used`: some clip has 4 columns.
All inputs are finite; a program needn't handle non-finite values.
Results may differ from the reference program's by a relative error of at most 0.0054.
Values may be sent and summed in bfloat16 or wider, within the bound.
A program may use at most 576 MiB of HBM per device.

```python
import jax
import jax.numpy as jnp
from jax import lax

CH = 256
FRAMES = 3
ROWS = 12
COLS = 4
TILES = 4
CLIPS = 4


def draw_neighbours(key, part):
    orders = jax.vmap(lambda single: jax.random.permutation(single, TILES))(jax.random.split(key, CLIPS)).astype(jnp.int32)
    clip_ids = jnp.arange(CLIPS, dtype=jnp.int32)[:, None]
    position = jnp.zeros((CLIPS, TILES), jnp.int32).at[clip_ids, orders].set(jnp.broadcast_to(jnp.arange(TILES, dtype=jnp.int32)[None, :], (CLIPS, TILES)))
    upper_tile = jnp.take_along_axis(orders, jnp.maximum(position - 1, 0), axis=1)
    upper_tile = jnp.where(position > 0, upper_tile, TILES)
    lower_tile = jnp.take_along_axis(orders, jnp.minimum(position + 1, TILES - 1), axis=1)
    lower_tile = jnp.where(position < TILES - 1, lower_tile, TILES)
    return jnp.stack([upper_tile, lower_tile], axis=-1).astype(jnp.int32)


def draw_rows_used(key, part):
    counts = jax.random.randint(key, (CLIPS, TILES), (ROWS + 3) // 4, ROWS + 1)
    chosen = jax.random.randint(jax.random.fold_in(key, 7), (CLIPS,), 0, TILES)
    tile_ids = jnp.arange(TILES, dtype=jnp.int32)[None, :]
    return jnp.where(tile_ids == chosen[:, None], ROWS, counts).astype(jnp.int32)


def draw_cols_used(key, part):
    counts = jax.random.randint(key, (CLIPS,), COLS // 2, COLS + 1)
    chosen = jax.random.randint(jax.random.fold_in(key, 11), (), 0, CLIPS)
    return jnp.where(jnp.arange(CLIPS, dtype=jnp.int32) == chosen, COLS, counts).astype(jnp.int32)


def steps_of(rng, shape, cuts, low, top_value):
    loudness = 1.0
    for dim, shards_of in cuts:
        heights = jax.random.uniform(jax.random.fold_in(jax.random.fold_in(rng, 6), dim), (shards_of,), jnp.float32, low / len(cuts), top_value / len(cuts))
        loudness = loudness * jnp.repeat(jnp.exp(heights), shape[dim] // shards_of).reshape((-1,) + (1,) * (len(shape) - 1 - dim))
    return loudness


def scatter_about(key, extent, width, limit, shards=(), held_as=jnp.bfloat16):
    values = jax.random.normal(key, extent, jnp.float32) * width
    if len(shards) > 0:
        values = steps_of(key, extent, shards, -0.22, 0.18) * values
    return jnp.clip(values, min=-limit, max=limit).astype(held_as)


def setup_inputs(seed: int = 0) -> dict:
    splits = jax.random.split(jax.random.key(seed), 7)
    video = scatter_about(splits[0], (CLIPS, TILES, FRAMES, ROWS, COLS, CH), 1.0, 6.0, ((0, 4), (1, 4)))
    cotangent = scatter_about(splits[1], (CLIPS, TILES, FRAMES, ROWS, COLS, CH), 1.0, 6.0, ((0, 4), (1, 4)))
    weights = scatter_about(splits[2], (2, 27, CH, CH), (27 * CH) ** -0.5, 0.078125, ((0, 2),))
    neighbours = draw_neighbours(jax.random.fold_in(splits[6], 71), 0)
    rows_used = draw_rows_used(jax.random.fold_in(splits[6], 71), 0)
    cols_used = draw_cols_used(jax.random.fold_in(splits[6], 71), 0)
    return {"video": video, "cotangent": cotangent, "weights": weights, "neighbours": neighbours, "rows_used": rows_used, "cols_used": cols_used}


def silu_grad(values):
    sigmoid = jax.nn.sigmoid(values)
    return sigmoid * (1.0 + values * (1.0 - sigmoid))

def pad_block(strip_field, upper, bottom, row_count):
    frame_count, height, columns, channels = strip_field.shape
    blank = jnp.zeros((frame_count, 1, columns, channels), strip_field.dtype)
    padded = jnp.concatenate([upper[:, None], strip_field, blank], axis=1)
    padded = lax.dynamic_update_slice_in_dim(padded, bottom[:, None], row_count + 1, axis=1)
    return jnp.pad(padded, ((0, 0), (0, 0), (1, 1), (0, 0)))

def patches(stacked, frame_count, height, columns):
    pieces = []
    for depth_off in range(3):
        for row_off in range(3):
            for col_off in range(3):
                pieces.append(stacked[depth_off:depth_off + frame_count, row_off:row_off + height, col_off:col_off + columns])
    return jnp.concatenate(pieces, axis=-1).reshape(frame_count * height * columns, -1)

def last_row(strip_field, row_count):
    return lax.dynamic_index_in_dim(strip_field, row_count - 1, axis=1, keepdims=False)

def one_clip(video, cotangent, weights, neighbours, rows_used, col_count):
    tile_count, frame_count, height, columns, channels = video.shape
    row_ids = jnp.arange(height, dtype=jnp.int32)
    col_ids = jnp.arange(columns, dtype=jnp.int32)
    inside = (row_ids[None, :, None] < rows_used[:, None, None]) & (col_ids[None, None, :] < col_count)
    inside_mask = inside[:, None, :, :, None]
    upper_tile = neighbours[:, 0]
    lower_tile = neighbours[:, 1]

    def halo_all(field):
        leading = field[:, :, 0]
        trailing = jax.vmap(last_row)(field, rows_used)
        upper = trailing[jnp.minimum(upper_tile, tile_count - 1)]
        upper = jnp.where((upper_tile < tile_count)[:, None, None, None], upper, jnp.zeros_like(upper))
        bottom = leading[jnp.minimum(lower_tile, tile_count - 1)]
        bottom = jnp.where((lower_tile < tile_count)[:, None, None, None], bottom, jnp.zeros_like(bottom))
        return jax.vmap(pad_block)(field, upper, bottom, rows_used)

    def tile_patches(stacked):
        return jax.vmap(lambda single: patches(single, frame_count, height, columns))(stacked).reshape(-1, 27 * channels)
    front_zero = jnp.zeros((tile_count, 2, height + 2, columns + 2, channels), jnp.bfloat16)
    forward_mats = [weights[index].reshape(27 * channels, channels) for index in range(2)]
    backward_mat = weights[1][::-1].transpose(0, 2, 1).reshape(27 * channels, channels)
    source = jnp.where(inside_mask, video, jnp.zeros_like(video)).astype(jnp.bfloat16)
    active_zero = jax.nn.silu(source.astype(jnp.float32)).astype(jnp.bfloat16)
    patch_zero = tile_patches(jnp.concatenate([front_zero, halo_all(active_zero)], axis=1))
    mixed = jnp.dot(patch_zero, forward_mats[0], preferred_element_type=jnp.float32).reshape(video.shape)
    hidden = jnp.where(inside_mask, source.astype(jnp.float32) + mixed, 0.0).astype(jnp.bfloat16)
    active_one = jax.nn.silu(hidden.astype(jnp.float32)).astype(jnp.bfloat16)
    patch_one = tile_patches(jnp.concatenate([front_zero, halo_all(active_one)], axis=1))
    mixed = jnp.dot(patch_one, forward_mats[1], preferred_element_type=jnp.float32).reshape(video.shape)
    decoded = jnp.where(inside_mask, hidden.astype(jnp.float32) + mixed, 0.0).astype(jnp.bfloat16)
    target = jnp.where(inside_mask, cotangent, jnp.zeros_like(cotangent)).astype(jnp.bfloat16)
    patch_back = tile_patches(jnp.concatenate([halo_all(target), front_zero], axis=1))
    spread = jnp.dot(patch_back, backward_mat, preferred_element_type=jnp.float32).reshape(video.shape)
    hidden_grad = jnp.where(inside_mask, target.astype(jnp.float32) + silu_grad(hidden.astype(jnp.float32)) * spread, 0.0).astype(jnp.bfloat16)
    grad_zero = jnp.dot(patch_zero.T, hidden_grad.reshape(-1, channels), preferred_element_type=jnp.float32)
    grad_one = jnp.dot(patch_one.T, target.reshape(-1, channels), preferred_element_type=jnp.float32)
    return (jnp.stack([hidden, decoded]), jnp.stack([grad_zero, grad_one]))

def reference(video, cotangent, weights, neighbours, rows_used, cols_used):

    def per_clip(total, inputs):
        clip_video, clip_cot, clip_nbrs, clip_rows, clip_cols = inputs
        outputs, clip_grads = one_clip(clip_video, clip_cot, weights, clip_nbrs, clip_rows, clip_cols)
        return (total + clip_grads, outputs)
    start = jnp.zeros((2, 27 * CH, CH), jnp.float32)
    total, sections = lax.scan(per_clip, start, (video, cotangent, neighbours, rows_used, cols_used))
    section_out = jnp.moveaxis(sections, 0, 1)
    grads = total.reshape(2, 3, 9 * CH * CH)
    return (section_out, grads)
```

```python
import jax
import jax.numpy as jnp
from jax import lax
from jax.sharding import PartitionSpec as P


def shifted(block, axis, distance):
    devices = range(lax.axis_size(axis))
    route = [(i - distance, i) for i in devices if i - distance in devices]
    return lax.ppermute(block, axis, route)


def silu_grad(values):
    sigmoid = jax.nn.sigmoid(values)
    return sigmoid * (1.0 + values * (1.0 - sigmoid))


def pad_block(strip_field, upper, bottom, row_count):
    frame_count, height, columns, channels = strip_field.shape
    blank = jnp.zeros((frame_count, 1, columns, channels), strip_field.dtype)
    padded = jnp.concatenate([upper[:, None], strip_field, blank], axis=1)
    padded = lax.dynamic_update_slice_in_dim(padded, bottom[:, None], row_count + 1, axis=1)
    return jnp.pad(padded, ((0, 0), (0, 0), (1, 1), (0, 0)))


def patches(stacked, frame_count, height, columns):
    pieces = []
    for depth_off in range(3):
        for row_off in range(3):
            for col_off in range(3):
                pieces.append(
                    stacked[
                        depth_off : depth_off + frame_count,
                        row_off : row_off + height,
                        col_off : col_off + columns,
                    ]
                )
    return jnp.concatenate(pieces, axis=-1).reshape(frame_count * height * columns, -1)


def own_entries(padded, weighting, axes):
    frame_count, tall, columns, channels = padded.shape
    height = tall - 2
    payload = jnp.concatenate([padded.reshape(-1, channels), weighting], axis=0)
    gathered = lax.all_gather(payload, axes, axis=0)
    cut = frame_count * tall * columns
    strips = gathered[:, :cut].reshape(-1, frame_count, tall, columns, channels)
    strips = jnp.pad(strips, ((0, 0), (2, 0), (0, 0), (1, 1), (0, 0)))
    upstream = gathered[:, cut:].reshape(-1, channels)
    row_total = 9 * channels // lax.axis_size(axes)
    start = lax.axis_index(axes) * row_total
    low = jnp.minimum(start // channels, 8)
    lower = []
    for step in range(-(-row_total // channels) + 1):
        tap = jnp.minimum(low + step, 8)
        lower.append(
            lax.dynamic_slice(
                strips,
                (0, 0, tap // 3, tap % 3, 0),
                (strips.shape[0], frame_count + 2, height, columns, channels),
            )
        )
    window = jnp.concatenate(lower, axis=-1)
    window = lax.dynamic_slice_in_dim(window, start - low * channels, row_total, 4)
    contract = (((0,), (0,)), ((), ()))
    return jnp.stack(
        [
            lax.dot_general(
                window[:, tap : tap + frame_count].reshape(-1, row_total),
                upstream,
                contract,
                preferred_element_type=jnp.float32,
            ).reshape(-1)
            for tap in range(3)
        ]
    )


def local(video, cotangent, weights, neighbours, rows_used, cols_used):
    window = video[0, 0]
    frame_count, height, columns, channels = window.shape
    tile_count = lax.axis_size("tile")
    section = lax.axis_index("segment")
    row_count = rows_used[0, 0]
    col_count = cols_used[0]
    upper_tile = neighbours[0, 0, 0]
    lower_tile = neighbours[0, 0, 1]
    row_ids = jnp.arange(height, dtype=jnp.int32)
    col_ids = jnp.arange(columns, dtype=jnp.int32)
    inside = (row_ids[:, None] < row_count) & (col_ids[None, :] < col_count)
    inside_mask = inside[None, :, :, None]
    kernel = weights[0]
    forward_mat = kernel.reshape(27 * channels, channels)
    backward_mat = kernel[::-1].transpose(0, 2, 1).reshape(27 * channels, channels)
    front_zero = jnp.zeros((2, height + 2, columns + 2, channels), jnp.bfloat16)

    def halo_block(field):
        leading = field[:, 0]
        trailing = lax.dynamic_index_in_dim(field, row_count - 1, axis=1, keepdims=False)
        both_rows = jnp.stack([leading, trailing], axis=1)
        gathered = lax.all_gather(both_rows[None], "tile", axis=0, tiled=True)
        upper = gathered[jnp.minimum(upper_tile, tile_count - 1), :, 1]
        bottom = gathered[jnp.minimum(lower_tile, tile_count - 1), :, 0]
        upper = jnp.where(upper_tile < tile_count, upper, jnp.zeros_like(upper))
        bottom = jnp.where(lower_tile < tile_count, bottom, jnp.zeros_like(bottom))
        return pad_block(field, upper, bottom, row_count)

    def advance(entry, history):
        count = entry.shape[0]
        activated = jax.nn.silu(entry.astype(jnp.float32)).astype(jnp.bfloat16)
        padded = halo_block(activated)
        stacked = jnp.concatenate([history, padded], axis=0)
        mixed = jnp.dot(
            patches(stacked, count, height, columns),
            forward_mat,
            preferred_element_type=jnp.float32,
        ).reshape(entry.shape)
        result = jnp.where(inside_mask, entry.astype(jnp.float32) + mixed, 0.0).astype(jnp.bfloat16)
        return (result, stacked[-2:], padded)

    source = jnp.where(inside_mask, window, jnp.zeros_like(window))
    is_encoder = section == 0
    first_out, first_hist, first_pad = advance(source, front_zero)
    latent = shifted(first_out, "segment", 1)
    second_out, second_hist, second_pad = advance(latent, front_zero)
    own_out = jnp.where(is_encoder, first_out, second_out)
    own_input = jnp.where(is_encoder, source, latent)
    own_pad = jnp.where(is_encoder, first_pad, second_pad)
    target = jnp.where(inside_mask, cotangent[0, 0], jnp.zeros_like(cotangent[0, 0]))
    back_stack = jnp.concatenate([halo_block(target), front_zero], axis=0)
    spread = jnp.dot(
        patches(back_stack, frame_count, height, columns),
        backward_mat,
        preferred_element_type=jnp.float32,
    ).reshape(target.shape)
    own_grad = jnp.where(
        inside_mask,
        target.astype(jnp.float32) + silu_grad(own_input.astype(jnp.float32)) * spread,
        0.0,
    ).astype(jnp.bfloat16)
    returned = shifted(own_grad, "segment", -1)
    weighting = jnp.where(is_encoder, returned, target).reshape(-1, channels)
    summed = own_entries(own_pad[:, :, 1:-1], weighting, ("clip", "tile"))
    return (own_out[None, None, None], summed[None])


def solution(mesh):
    in_specs = (
        P("clip", "tile", None, None, None, None),
        P("clip", "tile", None, None, None, None),
        P("segment", None, None, None),
        P("clip", "tile", None),
        P("clip", "tile"),
        P("clip"),
    )
    out_specs = (
        P("segment", "clip", "tile", None, None, None, None),
        P("segment", None, ("clip", "tile")),
    )
    return jax.shard_map(local, mesh=mesh, in_specs=in_specs, out_specs=out_specs, check_vma=False)
```

```python
import jax
import jax.numpy as jnp
from jax import lax
from jax.experimental import pallas as pl
from jax.experimental.pallas import tpu as pltpu
from jax.sharding import PartitionSpec as P


def shifted(block, axis, distance):
    devices = range(lax.axis_size(axis))
    route = [(i - distance, i) for i in devices if i - distance in devices]
    return lax.ppermute(block, axis, route)


def silu_grad(values):
    sigmoid = jax.nn.sigmoid(values)
    return sigmoid * (1.0 + values * (1.0 - sigmoid))


def pad_block(strip_field, upper, bottom, row_count):
    frame_count, height, columns, channels = strip_field.shape
    blank = jnp.zeros((frame_count, 1, columns, channels), strip_field.dtype)
    padded = jnp.concatenate([upper[:, None], strip_field, blank], axis=1)
    padded = lax.dynamic_update_slice_in_dim(padded, bottom[:, None], row_count + 1, axis=1)
    return jnp.pad(padded, ((0, 0), (0, 0), (1, 1), (0, 0)))


def patches(stacked, frame_count, height, columns):
    pieces = []
    for depth_off in range(3):
        for row_off in range(3):
            for col_off in range(3):
                pieces.append(
                    stacked[
                        depth_off : depth_off + frame_count,
                        row_off : row_off + height,
                        col_off : col_off + columns,
                    ]
                )
    return jnp.concatenate(pieces, axis=-1).reshape(frame_count * height * columns, -1)


def back_kernel(patch_ref, weight_ref, out_ref):
    taps, channels = weight_ref.shape[0], weight_ref.shape[2]
    total = jnp.zeros(out_ref.shape, jnp.float32)
    for tap in range(taps):
        total += lax.dot_general(
            patch_ref[:, tap * channels : (tap + 1) * channels],
            weight_ref[taps - 1 - tap],
            (((1,), (1,)), ((), ())),
            preferred_element_type=jnp.float32,
        )
    out_ref[...] = total


def conv_back_dot(patch_mat, kernel):
    rows, channels = patch_mat.shape[0], kernel.shape[1]
    return pl.pallas_call(
        back_kernel,
        out_shape=jax.ShapeDtypeStruct((rows, channels), jnp.float32),
        in_specs=[pl.BlockSpec(memory_space=pltpu.VMEM)] * 2,
        out_specs=pl.BlockSpec(memory_space=pltpu.VMEM),
        compiler_params=pltpu.CompilerParams(vmem_limit_bytes=24 * 2**20),
    )(patch_mat, kernel)


def own_entries(acts, ups, axes, frame_count, height, columns):
    strips, channels = acts.shape[0], acts.shape[-1]
    tall = acts.shape[1] // frame_count
    acts = acts.reshape(strips, frame_count, tall, channels)
    ups = ups.reshape(strips, frame_count, height * columns, channels)
    row_total = 9 * channels // lax.axis_size(axes)
    start = lax.axis_index(axes) * row_total
    low = jnp.minimum(start // channels, 8)
    lead = 16
    ups = jnp.pad(ups, ((0, 0), (0, 0), (lead, lead + tall - height * columns), (0, 0)))
    column = lax.broadcasted_iota(jnp.int32, (1, 1, ups.shape[2], 1), 2) % columns
    per_tap = []
    for step in range(-(-row_total // channels) + 1):
        tap = jnp.minimum(low + step, 8)
        row_off, col_off = tap // 3, tap % 3
        beside = column + col_off - 1
        held = jnp.where((beside >= 0) & (beside < columns), ups, jnp.zeros_like(ups))
        moved = lax.dynamic_slice_in_dim(held, lead - (columns * row_off + col_off - 1), tall, 2)
        per_tap.append(moved)
    contract = (((0, 1, 2), (0, 1, 2)), ((), ()))
    by_frame = []
    for tap in range(3):
        count = frame_count - 2 + tap
        entries = jnp.concatenate(
            [
                lax.dot_general(
                    acts[:, :count],
                    moved[:, frame_count - count :],
                    contract,
                    preferred_element_type=jnp.float32,
                )
                for moved in per_tap
            ],
            axis=0,
        )
        by_frame.append(
            lax.dynamic_slice_in_dim(entries, start - low * channels, row_total, 0).reshape(-1)
        )
    return jnp.stack(by_frame)


def local(video, cotangent, weights, neighbours, rows_used, cols_used):
    frame_count, height, columns, channels = video.shape[2:]
    tile_count = lax.axis_size("tile")
    section = lax.axis_index("segment")
    row_count = rows_used[0, 0]
    col_count = cols_used[0]
    upper_tile = neighbours[0, 0, 0]
    lower_tile = neighbours[0, 0, 1]
    row_ids = jnp.arange(height, dtype=jnp.int32)
    col_ids = jnp.arange(columns, dtype=jnp.int32)
    inside = (row_ids[:, None] < row_count) & (col_ids[None, :] < col_count)
    inside_mask = inside[None, :, :, None]
    kernel = weights[0]
    forward_mat = kernel.reshape(27 * channels, channels)
    front_zero = jnp.zeros((2, height + 2, columns + 2, channels), jnp.bfloat16)

    def halo_block(field):
        leading = field[:, 0]
        trailing = lax.dynamic_index_in_dim(field, row_count - 1, axis=1, keepdims=False)
        both_rows = jnp.stack([leading, trailing], axis=1)
        gathered = lax.all_gather(both_rows[None], "tile", axis=0, tiled=True)
        upper = gathered[jnp.minimum(upper_tile, tile_count - 1), :, 1]
        bottom = gathered[jnp.minimum(lower_tile, tile_count - 1), :, 0]
        upper = jnp.where(upper_tile < tile_count, upper, jnp.zeros_like(upper))
        bottom = jnp.where(lower_tile < tile_count, bottom, jnp.zeros_like(bottom))
        return pad_block(field, upper, bottom, row_count)

    def front(padded):
        stacked = jnp.concatenate([front_zero, padded], axis=0)
        patch_mat = patches(stacked, frame_count, height, columns)
        return jnp.dot(patch_mat, forward_mat, preferred_element_type=jnp.float32)

    def back(padded):
        stacked = jnp.concatenate([padded, front_zero], axis=0)
        return conv_back_dot(patches(stacked, frame_count, height, columns), kernel)

    def flat(field):
        rows = field.reshape(-1, channels)
        return jnp.pad(rows, ((0, frame_count * (height + 2) * columns - rows.shape[0]), (0, 0)))

    axes = ("clip", "tile")
    is_encoder = section == 0
    source = jnp.where(inside_mask, video[0, 0], 0).astype(jnp.bfloat16)
    target = jnp.where(inside_mask, cotangent[0, 0], 0).astype(jnp.bfloat16)
    active = jax.nn.silu(source.astype(jnp.float32)).astype(jnp.bfloat16)
    padded = halo_block(jnp.where(is_encoder, active, target))
    early = jnp.where(is_encoder, flat(padded[:, :, 1:-1]), flat(target))
    early_all = lax.all_gather(early, axes, axis=0)
    mixed = lax.cond(is_encoder, front, back, padded).reshape(target.shape)
    hidden = jnp.where(inside_mask, source.astype(jnp.float32) + mixed, 0.0).astype(jnp.bfloat16)
    latent = shifted(hidden, "segment", 1)
    wide = latent.astype(jnp.float32)
    own_grad = jnp.where(
        inside_mask, target.astype(jnp.float32) + silu_grad(wide) * mixed, 0.0
    ).astype(jnp.bfloat16)
    returned = shifted(own_grad, "segment", -1)
    padded_two = halo_block(jax.nn.silu(wide).astype(jnp.bfloat16))
    late = jnp.where(is_encoder, flat(returned), flat(padded_two[:, :, 1:-1]))
    late_all = lax.all_gather(late, axes, axis=0)
    decoded = jnp.where(
        inside_mask, wide + front(padded_two).reshape(target.shape), 0.0
    ).astype(jnp.bfloat16)
    own_out = jnp.where(is_encoder, hidden, decoded)
    acts = jnp.where(is_encoder, early_all, late_all)
    ups = jnp.where(is_encoder, late_all, early_all)[:, : frame_count * height * columns]
    summed = own_entries(acts, ups, axes, frame_count, height, columns)
    return (own_out[None, None, None], summed[None])


def solution(mesh):
    in_specs = (
        P("clip", "tile", None, None, None, None),
        P("clip", "tile", None, None, None, None),
        P("segment", None, None, None),
        P("clip", "tile", None),
        P("clip", "tile"),
        P("clip"),
    )
    out_specs = (
        P("segment", "clip", "tile", None, None, None, None),
        P("segment", None, ("clip", "tile")),
    )
    return jax.shard_map(local, mesh=mesh, in_specs=in_specs, out_specs=out_specs, check_vma=False)
```

```python
import functools

import jax
import jax.numpy as jnp
from jax import lax
from jax.experimental import pallas as pl
from jax.experimental.pallas import tpu as pltpu
from jax.sharding import PartitionSpec as P

MESH = pl.DeviceIdType.MESH


def shifted(block, axis, distance):
    devices = range(lax.axis_size(axis))
    route = [(i - distance, i) for i in devices if i - distance in devices]
    return lax.ppermute(block, axis, route)


def silu_grad(values):
    sigmoid = jax.nn.sigmoid(values)
    return sigmoid * (1.0 + values * (1.0 - sigmoid))


def pad_block(strip_field, upper, bottom, row_count):
    frame_count, height, columns, channels = strip_field.shape
    blank = jnp.zeros((frame_count, 1, columns, channels), strip_field.dtype)
    padded = jnp.concatenate([upper[:, None], strip_field, blank], axis=1)
    padded = lax.dynamic_update_slice_in_dim(padded, bottom[:, None], row_count + 1, axis=1)
    return jnp.pad(padded, ((0, 0), (0, 0), (1, 1), (0, 0)))


def conv_kernel(both, patch_ref, weight_ref, out_ref):
    taps, channels = weight_ref.shape[0], weight_ref.shape[2]
    rows = out_ref.shape[0]
    frame_rows = (patch_ref.shape[0] - rows) // 2

    def run(backward):
        total = jnp.zeros(out_ref.shape, jnp.float32)
        for tap in range(taps):
            low, place = tap // 9 * frame_rows, tap % 9 * channels
            total += lax.dot_general(
                patch_ref[low : low + rows, place : place + channels],
                weight_ref[taps - 1 - tap if backward else tap],
                (((1,), (1 if backward else 0,)), ((), ())),
                preferred_element_type=jnp.float32,
            )
        out_ref[...] = total

    if both:
        section = lax.axis_index("segment")
        pl.when(section == 0)(lambda: run(False))
        pl.when(section != 0)(lambda: run(True))
    else:
        run(False)


def conv_dot(patch_mat, kernel, both):
    channels = kernel.shape[1]
    rows = patch_mat.shape[0] * 3 // 5
    return pl.pallas_call(
        functools.partial(conv_kernel, both),
        out_shape=jax.ShapeDtypeStruct((rows, channels), jnp.float32),
        in_specs=[pl.BlockSpec(memory_space=pltpu.VMEM)] * 2,
        out_specs=pl.BlockSpec(memory_space=pltpu.VMEM),
        compiler_params=pltpu.CompilerParams(vmem_limit_bytes=24 * 2**20),
    )(patch_mat, kernel)


def spatial_patches(stacked, height, columns):
    pieces = [
        stacked[:, row_off : row_off + height, col_off : col_off + columns]
        for row_off in range(3)
        for col_off in range(3)
    ]
    return jnp.concatenate(pieces, axis=-1).reshape(stacked.shape[0] * height * columns, -1)


def gather_kernel(clips, tiles, own_ref, all_ref, send_sem, recv_sem, local_sem):
    section = lax.axis_index("segment")
    clip = lax.axis_index("clip")
    tile = lax.axis_index("tile")
    clip_peers = [lax.rem(clip + step, clips) for step in range(1, clips)]
    tile_peers = [lax.rem(tile + step, tiles) for step in range(1, tiles)]
    places = [(section, peer, tile) for peer in clip_peers]
    places += [(section, clip, peer) for peer in tile_peers]

    barrier = pltpu.get_barrier_semaphore()
    for place in places:
        pl.semaphore_signal(barrier, inc=1, device_id=place, device_id_type=MESH)
    pl.semaphore_wait(barrier, len(places))

    def send(source, slot_clip, number, place):
        copy = pltpu.make_async_remote_copy(
            src_ref=source,
            dst_ref=all_ref.at[slot_clip, tile],
            send_sem=send_sem.at[number],
            recv_sem=recv_sem.at[slot_clip, tile],
            device_id=place,
            device_id_type=MESH,
        )
        copy.start()
        return copy

    def arrived(slot_clip, slot_tile):
        slot = all_ref.at[slot_clip, slot_tile]
        pltpu.make_async_remote_copy(
            src_ref=slot,
            dst_ref=slot,
            send_sem=send_sem.at[0],
            recv_sem=recv_sem.at[slot_clip, slot_tile],
            device_id=places[0],
            device_id_type=MESH,
        ).wait_recv()

    own = pltpu.make_async_copy(own_ref, all_ref.at[clip, tile], local_sem)
    own.start()
    copies = [send(own_ref, clip, number, place) for number, place in enumerate(places)]
    for peer in clip_peers:
        arrived(peer, tile)
        for other in tile_peers:
            copies.append(send(all_ref.at[peer, tile], peer, len(copies), (section, clip, other)))
    for other in tile_peers:
        arrived(clip, other)
    for peer in clip_peers:
        for other in tile_peers:
            arrived(peer, other)
    own.wait()
    for copy in copies:
        copy.wait_send()


def gather_all(block):
    clips, tiles = lax.axis_size("clip"), lax.axis_size("tile")
    gathered = pl.pallas_call(
        functools.partial(gather_kernel, clips, tiles),
        out_shape=jax.ShapeDtypeStruct((clips, tiles) + block.shape, block.dtype),
        in_specs=[pl.BlockSpec(memory_space=pltpu.VMEM)],
        out_specs=pl.BlockSpec(memory_space=pltpu.VMEM),
        scratch_shapes=[
            pltpu.SemaphoreType.DMA((clips * tiles - 1,)),
            pltpu.SemaphoreType.DMA((clips, tiles)),
            pltpu.SemaphoreType.DMA,
        ],
        compiler_params=pltpu.CompilerParams(
            collective_id=0, has_side_effects=True, vmem_limit_bytes=32 * 2**20
        ),
    )(block)
    return gathered.reshape((clips * tiles,) + block.shape)


def own_entries(acts, ups, axes, frame_count, height, columns):
    strips, channels = acts.shape[0], acts.shape[-1]
    tall = acts.shape[1] // frame_count
    acts = acts.reshape(strips, frame_count, tall, channels)
    ups = ups.reshape(strips, frame_count, height * columns, channels)
    row_total = 9 * channels // lax.axis_size(axes)
    start = lax.axis_index(axes) * row_total
    low = jnp.minimum(start // channels, 8)
    lead = 16
    ups = jnp.pad(ups, ((0, 0), (0, 0), (lead, lead + tall - height * columns), (0, 0)))
    column = lax.broadcasted_iota(jnp.int32, (1, 1, ups.shape[2], 1), 2) % columns
    per_tap = []
    for step in range(-(-row_total // channels) + 1):
        tap = jnp.minimum(low + step, 8)
        row_off, col_off = tap // 3, tap % 3
        beside = column + col_off - 1
        held = jnp.where((beside >= 0) & (beside < columns), ups, jnp.zeros_like(ups))
        moved = lax.dynamic_slice_in_dim(held, lead - (columns * row_off + col_off - 1), tall, 2)
        per_tap.append(moved)
    contract = (((0, 1, 2), (0, 1, 2)), ((), ()))
    by_frame = []
    for tap in range(3):
        count = frame_count - 2 + tap
        entries = jnp.concatenate(
            [
                lax.dot_general(
                    acts[:, :count],
                    moved[:, frame_count - count :],
                    contract,
                    preferred_element_type=jnp.float32,
                )
                for moved in per_tap
            ],
            axis=0,
        )
        by_frame.append(
            lax.dynamic_slice_in_dim(entries, start - low * channels, row_total, 0).reshape(-1)
        )
    return jnp.stack(by_frame)


def local(video, cotangent, weights, neighbours, rows_used, cols_used):
    frame_count, height, columns, channels = video.shape[2:]
    tile_count = lax.axis_size("tile")
    section = lax.axis_index("segment")
    row_count = rows_used[0, 0]
    col_count = cols_used[0]
    upper_tile = neighbours[0, 0, 0]
    lower_tile = neighbours[0, 0, 1]
    row_ids = jnp.arange(height, dtype=jnp.int32)
    col_ids = jnp.arange(columns, dtype=jnp.int32)
    inside = (row_ids[:, None] < row_count) & (col_ids[None, :] < col_count)
    inside_mask = inside[None, :, :, None]
    kernel = weights[0]
    front_zero = jnp.zeros((2, height + 2, columns + 2, channels), jnp.bfloat16)

    def halo_block(field):
        leading = field[:, 0]
        trailing = lax.dynamic_index_in_dim(field, row_count - 1, axis=1, keepdims=False)
        both_rows = jnp.stack([leading, trailing], axis=1)
        gathered = lax.all_gather(both_rows[None], "tile", axis=0, tiled=True)
        upper = gathered[jnp.minimum(upper_tile, tile_count - 1), :, 1]
        bottom = gathered[jnp.minimum(lower_tile, tile_count - 1), :, 0]
        upper = jnp.where(upper_tile < tile_count, upper, jnp.zeros_like(upper))
        bottom = jnp.where(lower_tile < tile_count, bottom, jnp.zeros_like(bottom))
        return pad_block(field, upper, bottom, row_count)

    def flat(field):
        rows = field.reshape(-1, channels)
        return jnp.pad(rows, ((0, frame_count * (height + 2) * columns - rows.shape[0]), (0, 0)))

    axes = ("clip", "tile")
    is_encoder = section == 0
    source = jnp.where(inside_mask, video[0, 0], 0).astype(jnp.bfloat16)
    target = jnp.where(inside_mask, cotangent[0, 0], 0).astype(jnp.bfloat16)
    active = jax.nn.silu(source.astype(jnp.float32)).astype(jnp.bfloat16)
    padded = halo_block(jnp.where(is_encoder, active, target))
    early = jnp.where(is_encoder, flat(padded[:, :, 1:-1]), flat(target))
    early_all = lax.all_gather(early, axes, axis=0)
    stacked = jnp.where(
        is_encoder,
        jnp.concatenate([front_zero, padded], axis=0),
        jnp.concatenate([padded, front_zero], axis=0),
    )
    mixed = conv_dot(spatial_patches(stacked, height, columns), kernel, True).reshape(target.shape)
    hidden = jnp.where(inside_mask, source.astype(jnp.float32) + mixed, 0.0).astype(jnp.bfloat16)
    latent = shifted(hidden, "segment", 1)
    wide = latent.astype(jnp.float32)
    own_grad = jnp.where(
        inside_mask, target.astype(jnp.float32) + silu_grad(wide) * mixed, 0.0
    ).astype(jnp.bfloat16)
    returned = shifted(own_grad, "segment", -1)
    padded_two = halo_block(jax.nn.silu(wide).astype(jnp.bfloat16))
    late = jnp.where(is_encoder, flat(returned), flat(padded_two[:, :, 1:-1]))
    late_all = gather_all(late)
    stacked = jnp.concatenate([front_zero, padded_two], axis=0)
    second = conv_dot(spatial_patches(stacked, height, columns), kernel, False)
    decoded = jnp.where(
        inside_mask, wide + second.reshape(target.shape), 0.0
    ).astype(jnp.bfloat16)
    own_out = jnp.where(is_encoder, hidden, decoded)
    acts = jnp.where(is_encoder, early_all, late_all)
    ups = jnp.where(is_encoder, late_all, early_all)[:, : frame_count * height * columns]
    summed = own_entries(acts, ups, axes, frame_count, height, columns)
    return (own_out[None, None, None], summed[None])


def solution(mesh):
    in_specs = (
        P("clip", "tile", None, None, None, None),
        P("clip", "tile", None, None, None, None),
        P("segment", None, None, None),
        P("clip", "tile", None),
        P("clip", "tile"),
        P("clip"),
    )
    out_specs = (
        P("segment", "clip", "tile", None, None, None, None),
        P("segment", None, ("clip", "tile")),
    )
    return jax.shard_map(local, mesh=mesh, in_specs=in_specs, out_specs=out_specs, check_vma=False)
```

```python
import functools

import jax
import jax.numpy as jnp
from jax import lax
from jax.experimental import pallas as pl
from jax.experimental.pallas import tpu as pltpu
from jax.sharding import PartitionSpec as P

MESH = pl.DeviceIdType.MESH


def shifted(block, axis, distance):
    devices = range(lax.axis_size(axis))
    route = [(i - distance, i) for i in devices if i - distance in devices]
    return lax.ppermute(block, axis, route)


def silu_grad(values):
    sigmoid = jax.nn.sigmoid(values)
    return sigmoid * (1.0 + values * (1.0 - sigmoid))


def conv_kernel(both, columns, field_ref, weight_ref, out_ref, wide, taps_mat):
    taps, channels = weight_ref.shape[0], weight_ref.shape[2]
    rows = out_ref.shape[0]
    frame_rows = taps_mat.shape[1] // 5
    tall = frame_rows + 2 * columns
    field_rows = field_ref.shape[0]
    lead = 8

    def run(backward):
        wide[...] = jnp.zeros(wide.shape, jnp.float32)
        first = lead if backward else lead + 2 * tall
        wide[first : first + field_rows] = field_ref[...].astype(jnp.float32)
        column = lax.broadcasted_iota(jnp.int32, (frame_rows, channels), 0) % columns
        for frame in range(5):
            for row_off in range(3):
                for col_off in range(3):
                    start = lead + tall * frame + columns * row_off + col_off - 1
                    block = wide[start : start + frame_rows]
                    if col_off == 0:
                        block = jnp.where(column > 0, block, 0.0)
                    if col_off == 2:
                        block = jnp.where(column < columns - 1, block, 0.0)
                    taps_mat[
                        row_off,
                        frame_rows * frame : frame_rows * (frame + 1),
                        channels * col_off : channels * (col_off + 1),
                    ] = block.astype(jnp.bfloat16)
        total = jnp.zeros(out_ref.shape, jnp.float32)
        for depth_off in range(3):
            low = depth_off * frame_rows
            for row_off in range(3):
                tap = 9 * depth_off + 3 * row_off
                if not backward:
                    total += jnp.dot(
                        taps_mat[row_off, low : low + rows, :],
                        weight_ref[tap : tap + 3].reshape(3 * channels, channels),
                        preferred_element_type=jnp.float32,
                    )
                    continue
                for col_off in range(3):
                    total += lax.dot_general(
                        taps_mat[
                            row_off, low : low + rows, channels * col_off : channels * (col_off + 1)
                        ],
                        weight_ref[taps - 1 - tap - col_off],
                        (((1,), (1,)), ((), ())),
                        preferred_element_type=jnp.float32,
                    )
        out_ref[...] = total

    if both:
        section = lax.axis_index("segment")
        pl.when(section == 0)(lambda: run(False))
        pl.when(section != 0)(lambda: run(True))
    else:
        run(False)


def conv_dot(padded, kernel, rows, columns, both):
    channels = kernel.shape[1]
    frame_rows = rows // 3
    return pl.pallas_call(
        functools.partial(conv_kernel, both, columns),
        out_shape=jax.ShapeDtypeStruct((rows, channels), jnp.float32),
        in_specs=[pl.BlockSpec(memory_space=pltpu.VMEM)] * 2,
        out_specs=pl.BlockSpec(memory_space=pltpu.VMEM),
        scratch_shapes=[
            pltpu.VMEM((16 + 5 * (frame_rows + 2 * columns), channels), jnp.float32),
            pltpu.VMEM((3, 5 * frame_rows, 3 * channels), jnp.bfloat16),
        ],
        compiler_params=pltpu.CompilerParams(vmem_limit_bytes=24 * 2**20),
    )(padded, kernel)


def gather_kernel(clips, tiles, own_ref, all_ref, send_sem, recv_sem, local_sem):
    section = lax.axis_index("segment")
    clip = lax.axis_index("clip")
    tile = lax.axis_index("tile")
    clip_peers = [lax.rem(clip + step, clips) for step in range(1, clips)]
    tile_peers = [lax.rem(tile + step, tiles) for step in range(1, tiles)]
    places = [(section, peer, tile) for peer in clip_peers]
    places += [(section, clip, peer) for peer in tile_peers]

    barrier = pltpu.get_barrier_semaphore()
    for place in places:
        pl.semaphore_signal(barrier, inc=1, device_id=place, device_id_type=MESH)
    pl.semaphore_wait(barrier, len(places))

    def send(source, slot_clip, number, place):
        copy = pltpu.make_async_remote_copy(
            src_ref=source,
            dst_ref=all_ref.at[slot_clip, tile],
            send_sem=send_sem.at[number],
            recv_sem=recv_sem.at[slot_clip, tile],
            device_id=place,
            device_id_type=MESH,
        )
        copy.start()
        return copy

    def arrived(slot_clip, slot_tile):
        slot = all_ref.at[slot_clip, slot_tile]
        pltpu.make_async_remote_copy(
            src_ref=slot,
            dst_ref=slot,
            send_sem=send_sem.at[0],
            recv_sem=recv_sem.at[slot_clip, slot_tile],
            device_id=places[0],
            device_id_type=MESH,
        ).wait_recv()

    own = pltpu.make_async_copy(own_ref, all_ref.at[clip, tile], local_sem)
    own.start()
    copies = [send(own_ref, clip, number, place) for number, place in enumerate(places)]
    for peer in clip_peers:
        arrived(peer, tile)
        for other in tile_peers:
            copies.append(send(all_ref.at[peer, tile], peer, len(copies), (section, clip, other)))
    for other in tile_peers:
        arrived(clip, other)
    for peer in clip_peers:
        for other in tile_peers:
            arrived(peer, other)
    own.wait()
    for copy in copies:
        copy.wait_send()


def gather_all(block):
    clips, tiles = lax.axis_size("clip"), lax.axis_size("tile")
    gathered = pl.pallas_call(
        functools.partial(gather_kernel, clips, tiles),
        out_shape=jax.ShapeDtypeStruct((clips, tiles) + block.shape, block.dtype),
        in_specs=[pl.BlockSpec(memory_space=pltpu.VMEM)],
        out_specs=pl.BlockSpec(memory_space=pltpu.VMEM),
        scratch_shapes=[
            pltpu.SemaphoreType.DMA((clips * tiles - 1,)),
            pltpu.SemaphoreType.DMA((clips, tiles)),
            pltpu.SemaphoreType.DMA,
        ],
        compiler_params=pltpu.CompilerParams(
            collective_id=0, has_side_effects=True, vmem_limit_bytes=32 * 2**20
        ),
    )(block)
    return gathered.reshape((clips * tiles,) + block.shape)


def own_entries(acts, ups, axes, frame_count, height, columns):
    strips, channels = acts.shape[0], acts.shape[-1]
    tall = acts.shape[1] // frame_count
    acts = acts.reshape(strips, frame_count, tall, channels)
    ups = ups.reshape(strips, frame_count, height * columns, channels)
    row_total = 9 * channels // lax.axis_size(axes)
    start = lax.axis_index(axes) * row_total
    low = jnp.minimum(start // channels, 8)
    lead = 16
    ups = jnp.pad(ups, ((0, 0), (0, 0), (lead, lead + tall - height * columns), (0, 0)))
    column = lax.broadcasted_iota(jnp.int32, (1, 1, ups.shape[2], 1), 2) % columns
    per_tap = []
    for step in range(-(-row_total // channels) + 1):
        tap = jnp.minimum(low + step, 8)
        row_off, col_off = tap // 3, tap % 3
        beside = column + col_off - 1
        held = jnp.where((beside >= 0) & (beside < columns), ups, jnp.zeros_like(ups))
        moved = lax.dynamic_slice_in_dim(held, lead - (columns * row_off + col_off - 1), tall, 2)
        per_tap.append(moved)
    contract = (((0, 1, 2), (0, 1, 2)), ((), ()))
    by_frame = []
    for tap in range(3):
        count = frame_count - 2 + tap
        entries = jnp.concatenate(
            [
                lax.dot_general(
                    acts[:, :count],
                    moved[:, frame_count - count :],
                    contract,
                    preferred_element_type=jnp.float32,
                )
                for moved in per_tap
            ],
            axis=0,
        )
        by_frame.append(
            lax.dynamic_slice_in_dim(entries, start - low * channels, row_total, 0).reshape(-1)
        )
    return jnp.stack(by_frame)


def local(video, cotangent, weights, neighbours, rows_used, cols_used):
    frame_count, height, columns, channels = video.shape[2:]
    tile_count = lax.axis_size("tile")
    section = lax.axis_index("segment")
    row_count = rows_used[0, 0]
    col_count = cols_used[0]
    upper_tile = neighbours[0, 0, 0]
    lower_tile = neighbours[0, 0, 1]
    rows = frame_count * height * columns
    tall = (height + 2) * columns
    ids = lax.broadcasted_iota(jnp.int32, (rows, 1), 0)
    inside = (ids // columns % height < row_count) & (ids % columns < col_count)
    kernel = weights[0]

    def halo_block(field):
        frames = field.reshape(frame_count, height * columns, channels)
        leading = frames[:, :columns]
        trailing = lax.dynamic_slice_in_dim(frames, (row_count - 1) * columns, columns, 1)
        both_rows = jnp.stack([leading, trailing], axis=1)
        gathered = lax.all_gather(both_rows[None], "tile", axis=0, tiled=True)
        upper = gathered[jnp.minimum(upper_tile, tile_count - 1), :, 1]
        bottom = gathered[jnp.minimum(lower_tile, tile_count - 1), :, 0]
        upper = jnp.where(upper_tile < tile_count, upper, jnp.zeros_like(upper))
        bottom = jnp.where(lower_tile < tile_count, bottom, jnp.zeros_like(bottom))
        padded = jnp.concatenate([upper, frames, jnp.zeros_like(upper)], axis=1)
        padded = lax.dynamic_update_slice_in_dim(padded, bottom, (row_count + 1) * columns, axis=1)
        return padded.reshape(frame_count * tall, channels)

    def flat(field):
        return jnp.pad(field, ((0, frame_count * tall - rows), (0, 0)))

    axes = ("clip", "tile")
    is_encoder = section == 0
    source = jnp.where(inside, video.reshape(rows, channels), 0).astype(jnp.bfloat16)
    target = jnp.where(inside, cotangent.reshape(rows, channels), 0).astype(jnp.bfloat16)
    active = jax.nn.silu(source.astype(jnp.float32)).astype(jnp.bfloat16)
    padded = halo_block(jnp.where(is_encoder, active, target))
    early = jnp.where(is_encoder, padded, flat(target))
    early_all = lax.all_gather(early, axes, axis=0)
    mixed = conv_dot(padded, kernel, rows, columns, True)
    hidden = jnp.where(inside, source.astype(jnp.float32) + mixed, 0.0).astype(jnp.bfloat16)
    latent = shifted(hidden, "segment", 1)
    wide = latent.astype(jnp.float32)
    own_grad = jnp.where(
        inside, target.astype(jnp.float32) + silu_grad(wide) * mixed, 0.0
    ).astype(jnp.bfloat16)
    returned = shifted(own_grad, "segment", -1)
    padded_two = halo_block(jax.nn.silu(wide).astype(jnp.bfloat16))
    late = jnp.where(is_encoder, flat(returned), padded_two)
    late_all = gather_all(late)
    second = conv_dot(padded_two, kernel, rows, columns, False)
    decoded = jnp.where(inside, wide + second, 0.0).astype(jnp.bfloat16)
    own_out = jnp.where(is_encoder, hidden, decoded).reshape(video.shape[2:])
    acts = jnp.where(is_encoder, early_all, late_all)
    ups = jnp.where(is_encoder, late_all, early_all)[:, :rows]
    summed = own_entries(acts, ups, axes, frame_count, height, columns)
    return (own_out[None, None, None], summed[None])


def solution(mesh):
    in_specs = (
        P("clip", "tile", None, None, None, None),
        P("clip", "tile", None, None, None, None),
        P("segment", None, None, None),
        P("clip", "tile", None),
        P("clip", "tile"),
        P("clip"),
    )
    out_specs = (
        P("segment", "clip", "tile", None, None, None, None),
        P("segment", None, ("clip", "tile")),
    )
    return jax.shard_map(local, mesh=mesh, in_specs=in_specs, out_specs=out_specs, check_vma=False)
```

```python
import functools

import jax
import jax.numpy as jnp
from jax import lax
from jax.experimental import pallas as pl
from jax.experimental.pallas import tpu as pltpu
from jax.sharding import PartitionSpec as P

MESH = pl.DeviceIdType.MESH


def shifted(block, axis, distance):
    devices = range(lax.axis_size(axis))
    route = [(i - distance, i) for i in devices if i - distance in devices]
    return lax.ppermute(block, axis, route)


def silu_grad(values):
    sigmoid = jax.nn.sigmoid(values)
    return sigmoid * (1.0 + values * (1.0 - sigmoid))


def conv_kernel(both, columns, field_ref, weight_ref, out_ref, wide, taps_mat):
    taps, channels = weight_ref.shape[0], weight_ref.shape[2]
    rows = out_ref.shape[0]
    frame_rows = taps_mat.shape[1] // 5
    tall = frame_rows + 2 * columns
    field_rows = field_ref.shape[0]
    lead = 8

    def run(backward):
        wide[...] = jnp.zeros(wide.shape, jnp.float32)
        first = lead if backward else lead + 2 * tall
        wide[first : first + field_rows] = field_ref[...].astype(jnp.float32)
        column = lax.broadcasted_iota(jnp.int32, (frame_rows, channels), 0) % columns
        for frame in range(5):
            for row_off in range(3):
                for col_off in range(3):
                    start = lead + tall * frame + columns * row_off + col_off - 1
                    block = wide[start : start + frame_rows]
                    if col_off == 0:
                        block = jnp.where(column > 0, block, 0.0)
                    if col_off == 2:
                        block = jnp.where(column < columns - 1, block, 0.0)
                    taps_mat[
                        row_off,
                        frame_rows * frame : frame_rows * (frame + 1),
                        channels * col_off : channels * (col_off + 1),
                    ] = block.astype(jnp.bfloat16)
        total = jnp.zeros(out_ref.shape, jnp.float32)
        for depth_off in range(3):
            low = depth_off * frame_rows
            for row_off in range(3):
                tap = 9 * depth_off + 3 * row_off
                if not backward:
                    total += jnp.dot(
                        taps_mat[row_off, low : low + rows, :],
                        weight_ref[tap : tap + 3].reshape(3 * channels, channels),
                        preferred_element_type=jnp.float32,
                    )
                    continue
                for col_off in range(3):
                    total += lax.dot_general(
                        taps_mat[
                            row_off, low : low + rows, channels * col_off : channels * (col_off + 1)
                        ],
                        weight_ref[taps - 1 - tap - col_off],
                        (((1,), (1,)), ((), ())),
                        preferred_element_type=jnp.float32,
                    )
        out_ref[...] = total

    if both:
        section = lax.axis_index("segment")
        pl.when(section == 0)(lambda: run(False))
        pl.when(section != 0)(lambda: run(True))
    else:
        run(False)


def conv_dot(padded, kernel, rows, columns, both):
    channels = kernel.shape[1]
    frame_rows = rows // 3
    return pl.pallas_call(
        functools.partial(conv_kernel, both, columns),
        out_shape=jax.ShapeDtypeStruct((rows, channels), jnp.float32),
        in_specs=[pl.BlockSpec(memory_space=pltpu.VMEM)] * 2,
        out_specs=pl.BlockSpec(memory_space=pltpu.VMEM),
        scratch_shapes=[
            pltpu.VMEM((16 + 5 * (frame_rows + 2 * columns), channels), jnp.float32),
            pltpu.VMEM((3, 5 * frame_rows, 3 * channels), jnp.bfloat16),
        ],
        compiler_params=pltpu.CompilerParams(vmem_limit_bytes=24 * 2**20),
        cost_estimate=pl.CostEstimate(flops=0, bytes_accessed=4096, transcendentals=0),
    )(padded, kernel)


def gather_kernel(clips, tiles, own_ref, all_ref, send_sem, recv_sem, local_sem):
    section = lax.axis_index("segment")
    clip = lax.axis_index("clip")
    tile = lax.axis_index("tile")
    clip_peers = [lax.rem(clip + step, clips) for step in range(1, clips)]
    tile_peers = [lax.rem(tile + step, tiles) for step in range(1, tiles)]
    places = [(section, peer, tile) for peer in clip_peers]
    places += [(section, clip, peer) for peer in tile_peers]

    barrier = pltpu.get_barrier_semaphore()
    for place in places:
        pl.semaphore_signal(barrier, inc=1, device_id=place, device_id_type=MESH)
    pl.semaphore_wait(barrier, len(places))

    def send(source, slot_clip, number, place):
        copy = pltpu.make_async_remote_copy(
            src_ref=source,
            dst_ref=all_ref.at[slot_clip, tile],
            send_sem=send_sem.at[number],
            recv_sem=recv_sem.at[slot_clip, tile],
            device_id=place,
            device_id_type=MESH,
        )
        copy.start()
        return copy

    def arrived(slot_clip, slot_tile):
        slot = all_ref.at[slot_clip, slot_tile]
        pltpu.make_async_remote_copy(
            src_ref=slot,
            dst_ref=slot,
            send_sem=send_sem.at[0],
            recv_sem=recv_sem.at[slot_clip, slot_tile],
            device_id=places[0],
            device_id_type=MESH,
        ).wait_recv()

    own = pltpu.make_async_copy(own_ref, all_ref.at[clip, tile], local_sem)
    own.start()
    copies = [send(own_ref, clip, number, place) for number, place in enumerate(places)]
    for peer in clip_peers:
        arrived(peer, tile)
        for other in tile_peers:
            copies.append(send(all_ref.at[peer, tile], peer, len(copies), (section, clip, other)))
    for other in tile_peers:
        arrived(clip, other)
    for peer in clip_peers:
        for other in tile_peers:
            arrived(peer, other)
    own.wait()
    for copy in copies:
        copy.wait_send()


def gather_all(block):
    clips, tiles = lax.axis_size("clip"), lax.axis_size("tile")
    gathered = pl.pallas_call(
        functools.partial(gather_kernel, clips, tiles),
        out_shape=jax.ShapeDtypeStruct((clips, tiles) + block.shape, block.dtype),
        in_specs=[pl.BlockSpec(memory_space=pltpu.VMEM)],
        out_specs=pl.BlockSpec(memory_space=pltpu.VMEM),
        scratch_shapes=[
            pltpu.SemaphoreType.DMA((clips * tiles - 1,)),
            pltpu.SemaphoreType.DMA((clips, tiles)),
            pltpu.SemaphoreType.DMA,
        ],
        compiler_params=pltpu.CompilerParams(
            collective_id=0, has_side_effects=True, vmem_limit_bytes=32 * 2**20
        ),
        cost_estimate=pl.CostEstimate(flops=0, bytes_accessed=4096, transcendentals=0),
    )(block)
    return gathered.reshape((clips * tiles,) + block.shape)


def own_entries(acts, ups, axes, frame_count, height, columns):
    strips, channels = acts.shape[0], acts.shape[-1]
    tall = acts.shape[1] // frame_count
    acts = acts.reshape(strips, frame_count, tall, channels)
    ups = ups.reshape(strips, frame_count, height * columns, channels)
    row_total = 9 * channels // lax.axis_size(axes)
    start = lax.axis_index(axes) * row_total
    low = jnp.minimum(start // channels, 8)
    lead = 16
    ups = jnp.pad(ups, ((0, 0), (0, 0), (lead, lead + tall - height * columns), (0, 0)))
    column = lax.broadcasted_iota(jnp.int32, (1, 1, ups.shape[2], 1), 2) % columns
    per_tap = []
    for step in range(-(-row_total // channels) + 1):
        tap = jnp.minimum(low + step, 8)
        row_off, col_off = tap // 3, tap % 3
        beside = column + col_off - 1
        held = jnp.where((beside >= 0) & (beside < columns), ups, jnp.zeros_like(ups))
        moved = lax.dynamic_slice_in_dim(held, lead - (columns * row_off + col_off - 1), tall, 2)
        per_tap.append(moved)
    contract = (((0, 1, 2), (0, 1, 2)), ((), ()))
    by_frame = []
    for tap in range(3):
        count = frame_count - 2 + tap
        entries = jnp.concatenate(
            [
                lax.dot_general(
                    acts[:, :count],
                    moved[:, frame_count - count :],
                    contract,
                    preferred_element_type=jnp.float32,
                )
                for moved in per_tap
            ],
            axis=0,
        )
        by_frame.append(
            lax.dynamic_slice_in_dim(entries, start - low * channels, row_total, 0).reshape(-1)
        )
    return jnp.stack(by_frame)


def local(video, cotangent, weights, neighbours, rows_used, cols_used):
    frame_count, height, columns, channels = video.shape[2:]
    tile_count = lax.axis_size("tile")
    section = lax.axis_index("segment")
    row_count = rows_used[0, 0]
    col_count = cols_used[0]
    upper_tile = neighbours[0, 0, 0]
    lower_tile = neighbours[0, 0, 1]
    rows = frame_count * height * columns
    tall = (height + 2) * columns
    ids = lax.broadcasted_iota(jnp.int32, (rows, 1), 0)
    inside = (ids // columns % height < row_count) & (ids % columns < col_count)
    kernel = weights[0]

    def halo_block(field):
        frames = field.reshape(frame_count, height * columns, channels)
        leading = frames[:, :columns]
        trailing = lax.dynamic_slice_in_dim(frames, (row_count - 1) * columns, columns, 1)
        both_rows = jnp.stack([leading, trailing], axis=1)
        gathered = lax.all_gather(both_rows[None], "tile", axis=0, tiled=True)
        upper = gathered[jnp.minimum(upper_tile, tile_count - 1), :, 1]
        bottom = gathered[jnp.minimum(lower_tile, tile_count - 1), :, 0]
        upper = jnp.where(upper_tile < tile_count, upper, jnp.zeros_like(upper))
        bottom = jnp.where(lower_tile < tile_count, bottom, jnp.zeros_like(bottom))
        padded = jnp.concatenate([upper, frames, jnp.zeros_like(upper)], axis=1)
        padded = lax.dynamic_update_slice_in_dim(padded, bottom, (row_count + 1) * columns, axis=1)
        return padded.reshape(frame_count * tall, channels)

    def flat(field):
        return jnp.pad(field, ((0, frame_count * tall - rows), (0, 0)))

    axes = ("clip", "tile")
    is_encoder = section == 0
    source = jnp.where(inside, video.reshape(rows, channels), 0).astype(jnp.bfloat16)
    target = jnp.where(inside, cotangent.reshape(rows, channels), 0).astype(jnp.bfloat16)
    active = jax.nn.silu(source.astype(jnp.float32)).astype(jnp.bfloat16)
    padded = halo_block(jnp.where(is_encoder, active, target))
    early = jnp.where(is_encoder, padded, flat(target))
    early, padded = lax.optimization_barrier((early, padded))
    early_all = lax.all_gather(early, axes, axis=0)
    mixed = conv_dot(padded, kernel, rows, columns, True)
    hidden = jnp.where(inside, source.astype(jnp.float32) + mixed, 0.0).astype(jnp.bfloat16)
    latent = shifted(hidden, "segment", 1)
    wide = latent.astype(jnp.float32)
    own_grad = jnp.where(
        inside, target.astype(jnp.float32) + silu_grad(wide) * mixed, 0.0
    ).astype(jnp.bfloat16)
    returned = shifted(own_grad, "segment", -1)
    padded_two = halo_block(jax.nn.silu(wide).astype(jnp.bfloat16))
    late = jnp.where(is_encoder, flat(returned), padded_two)
    late_all = gather_all(late)
    second = conv_dot(padded_two, kernel, rows, columns, False)
    decoded = jnp.where(inside, wide + second, 0.0).astype(jnp.bfloat16)
    own_out = jnp.where(is_encoder, hidden, decoded).reshape(video.shape[2:])
    acts = jnp.where(is_encoder, early_all, late_all)
    ups = jnp.where(is_encoder, late_all, early_all)[:, :rows]
    summed = own_entries(acts, ups, axes, frame_count, height, columns)
    return (own_out[None, None, None], summed[None])


def solution(mesh):
    in_specs = (
        P("clip", "tile", None, None, None, None),
        P("clip", "tile", None, None, None, None),
        P("segment", None, None, None),
        P("clip", "tile", None),
        P("clip", "tile"),
        P("clip"),
    )
    out_specs = (
        P("segment", "clip", "tile", None, None, None, None),
        P("segment", None, ("clip", "tile")),
    )
    return jax.shard_map(local, mesh=mesh, in_specs=in_specs, out_specs=out_specs, check_vma=False)
```

```python
import functools

import jax
import jax.numpy as jnp
from jax import lax
from jax.experimental import pallas as pl
from jax.experimental.pallas import tpu as pltpu
from jax.sharding import PartitionSpec as P

MESH = pl.DeviceIdType.MESH


def shifted(block, axis, distance):
    devices = range(lax.axis_size(axis))
    route = [(i - distance, i) for i in devices if i - distance in devices]
    return lax.ppermute(block, axis, route)


def silu_grad(values):
    sigmoid = jax.nn.sigmoid(values)
    return sigmoid * (1.0 + values * (1.0 - sigmoid))


def conv_kernel(both, columns, field_ref, weight_ref, out_ref, wide, taps_mat):
    taps, channels = weight_ref.shape[0], weight_ref.shape[2]
    rows = out_ref.shape[0]
    frame_rows = taps_mat.shape[1] // 5
    tall = frame_rows + 2 * columns
    field_rows = field_ref.shape[0]
    lead = 8

    def run(backward):
        wide[...] = jnp.zeros(wide.shape, jnp.float32)
        first = lead if backward else lead + 2 * tall
        wide[first : first + field_rows] = field_ref[...].astype(jnp.float32)
        column = lax.broadcasted_iota(jnp.int32, (frame_rows, channels), 0) % columns
        for frame in range(5):
            for row_off in range(3):
                for col_off in range(3):
                    start = lead + tall * frame + columns * row_off + col_off - 1
                    block = wide[start : start + frame_rows]
                    if col_off == 0:
                        block = jnp.where(column > 0, block, 0.0)
                    if col_off == 2:
                        block = jnp.where(column < columns - 1, block, 0.0)
                    taps_mat[
                        row_off,
                        frame_rows * frame : frame_rows * (frame + 1),
                        channels * col_off : channels * (col_off + 1),
                    ] = block.astype(jnp.bfloat16)
        total = jnp.zeros(out_ref.shape, jnp.float32)
        for depth_off in range(3):
            low = depth_off * frame_rows
            for row_off in range(3):
                tap = 9 * depth_off + 3 * row_off
                if not backward:
                    total += jnp.dot(
                        taps_mat[row_off, low : low + rows, :],
                        weight_ref[tap : tap + 3].reshape(3 * channels, channels),
                        preferred_element_type=jnp.float32,
                    )
                    continue
                for col_off in range(3):
                    total += lax.dot_general(
                        taps_mat[
                            row_off, low : low + rows, channels * col_off : channels * (col_off + 1)
                        ],
                        weight_ref[taps - 1 - tap - col_off],
                        (((1,), (1,)), ((), ())),
                        preferred_element_type=jnp.float32,
                    )
        out_ref[...] = total

    if both:
        section = lax.axis_index("segment")
        pl.when(section == 0)(lambda: run(False))
        pl.when(section != 0)(lambda: run(True))
    else:
        run(False)


def conv_dot(padded, kernel, rows, columns, both):
    channels = kernel.shape[1]
    frame_rows = rows // 3
    return pl.pallas_call(
        functools.partial(conv_kernel, both, columns),
        out_shape=jax.ShapeDtypeStruct((rows, channels), jnp.float32),
        in_specs=[pl.BlockSpec(memory_space=pltpu.VMEM)] * 2,
        out_specs=pl.BlockSpec(memory_space=pltpu.VMEM),
        scratch_shapes=[
            pltpu.VMEM((16 + 5 * (frame_rows + 2 * columns), channels), jnp.float32),
            pltpu.VMEM((3, 5 * frame_rows, 3 * channels), jnp.bfloat16),
        ],
        compiler_params=pltpu.CompilerParams(vmem_limit_bytes=24 * 2**20),
        cost_estimate=pl.CostEstimate(flops=0, bytes_accessed=4096, transcendentals=0),
    )(padded, kernel)


def gather_kernel(clips, tiles, own_ref, all_ref, send_sem, recv_sem, local_sem):
    section = lax.axis_index("segment")
    clip = lax.axis_index("clip")
    tile = lax.axis_index("tile")
    clip_peers = [lax.rem(clip + step, clips) for step in range(1, clips)]
    tile_peers = [lax.rem(tile + step, tiles) for step in range(1, tiles)]
    places = [(section, peer, tile) for peer in clip_peers]
    places += [(section, clip, peer) for peer in tile_peers]

    barrier = pltpu.get_barrier_semaphore()
    for place in places:
        pl.semaphore_signal(barrier, inc=1, device_id=place, device_id_type=MESH)
    pl.semaphore_wait(barrier, len(places))

    def send(source, slot_clip, number, place):
        copy = pltpu.make_async_remote_copy(
            src_ref=source,
            dst_ref=all_ref.at[slot_clip, tile],
            send_sem=send_sem.at[number],
            recv_sem=recv_sem.at[slot_clip, tile],
            device_id=place,
            device_id_type=MESH,
        )
        copy.start()
        return copy

    def arrived(slot_clip, slot_tile):
        slot = all_ref.at[slot_clip, slot_tile]
        pltpu.make_async_remote_copy(
            src_ref=slot,
            dst_ref=slot,
            send_sem=send_sem.at[0],
            recv_sem=recv_sem.at[slot_clip, slot_tile],
            device_id=places[0],
            device_id_type=MESH,
        ).wait_recv()

    own = pltpu.make_async_copy(own_ref, all_ref.at[clip, tile], local_sem)
    own.start()
    copies = [send(own_ref, clip, number, place) for number, place in enumerate(places)]
    for peer in clip_peers:
        arrived(peer, tile)
        for other in tile_peers:
            copies.append(send(all_ref.at[peer, tile], peer, len(copies), (section, clip, other)))
    for other in tile_peers:
        arrived(clip, other)
    for peer in clip_peers:
        for other in tile_peers:
            arrived(peer, other)
    own.wait()
    for copy in copies:
        copy.wait_send()


def gather_all(block):
    clips, tiles = lax.axis_size("clip"), lax.axis_size("tile")
    gathered = pl.pallas_call(
        functools.partial(gather_kernel, clips, tiles),
        out_shape=jax.ShapeDtypeStruct((clips, tiles) + block.shape, block.dtype),
        in_specs=[pl.BlockSpec(memory_space=pltpu.VMEM)],
        out_specs=pl.BlockSpec(memory_space=pltpu.VMEM),
        scratch_shapes=[
            pltpu.SemaphoreType.DMA((clips * tiles - 1,)),
            pltpu.SemaphoreType.DMA((clips, tiles)),
            pltpu.SemaphoreType.DMA,
        ],
        compiler_params=pltpu.CompilerParams(
            collective_id=0, has_side_effects=True, vmem_limit_bytes=32 * 2**20
        ),
        cost_estimate=pl.CostEstimate(flops=0, bytes_accessed=4096, transcendentals=0),
    )(block)
    return gathered.reshape((clips * tiles,) + block.shape)


def own_entries(acts, ups, axes, frame_count, height, columns):
    strips, channels = acts.shape[0], acts.shape[-1]
    tall = acts.shape[1] // frame_count
    acts = acts.reshape(strips, frame_count, tall, channels)
    ups = ups.reshape(strips, frame_count, height * columns, channels)
    row_total = 9 * channels // lax.axis_size(axes)
    start = lax.axis_index(axes) * row_total
    low = jnp.minimum(start // channels, 8)
    lead = 16
    ups = jnp.pad(ups, ((0, 0), (0, 0), (lead, lead + tall - height * columns), (0, 0)))
    column = lax.broadcasted_iota(jnp.int32, (1, 1, ups.shape[2], 1), 2) % columns
    per_tap = []
    for step in range(-(-row_total // channels) + 1):
        tap = jnp.minimum(low + step, 8)
        row_off, col_off = tap // 3, tap % 3
        beside = column + col_off - 1
        held = jnp.where((beside >= 0) & (beside < columns), ups, jnp.zeros_like(ups))
        moved = lax.dynamic_slice_in_dim(held, lead - (columns * row_off + col_off - 1), tall, 2)
        per_tap.append(moved)
    contract = (((0, 1, 2), (0, 1, 2)), ((), ()))
    by_frame = []
    for tap in range(3):
        count = frame_count - 2 + tap
        entries = jnp.concatenate(
            [
                lax.dot_general(
                    acts[:, :count],
                    moved[:, frame_count - count :],
                    contract,
                    preferred_element_type=jnp.float32,
                )
                for moved in per_tap
            ],
            axis=0,
        )
        by_frame.append(
            lax.dynamic_slice_in_dim(entries, start - low * channels, row_total, 0).reshape(-1)
        )
    return jnp.stack(by_frame)


def local(video, cotangent, weights, neighbours, rows_used, cols_used):
    frame_count, height, columns, channels = video.shape[2:]
    tile_count = lax.axis_size("tile")
    section = lax.axis_index("segment")
    row_count = rows_used[0, 0]
    col_count = cols_used[0]
    upper_tile = neighbours[0, 0, 0]
    lower_tile = neighbours[0, 0, 1]
    rows = frame_count * height * columns
    tall = (height + 2) * columns
    ids = lax.broadcasted_iota(jnp.int32, (rows, 1), 0)
    inside = (ids // columns % height < row_count) & (ids % columns < col_count)
    kernel = weights[0]

    def halo_block(field):
        frames = field.reshape(frame_count, height * columns, channels)
        leading = frames[:, :columns]
        trailing = lax.dynamic_slice_in_dim(frames, (row_count - 1) * columns, columns, 1)
        both_rows = jnp.stack([leading, trailing], axis=1)
        gathered = lax.all_gather(both_rows[None], "tile", axis=0, tiled=True)
        upper = gathered[jnp.minimum(upper_tile, tile_count - 1), :, 1]
        bottom = gathered[jnp.minimum(lower_tile, tile_count - 1), :, 0]
        upper = jnp.where(upper_tile < tile_count, upper, jnp.zeros_like(upper))
        bottom = jnp.where(lower_tile < tile_count, bottom, jnp.zeros_like(bottom))
        padded = jnp.concatenate([upper, frames, jnp.zeros_like(upper)], axis=1)
        padded = lax.dynamic_update_slice_in_dim(padded, bottom, (row_count + 1) * columns, axis=1)
        return padded.reshape(frame_count * tall, channels)

    def flat(field):
        return jnp.pad(field, ((0, frame_count * tall - rows), (0, 0)))

    axes = ("clip", "tile")
    is_encoder = section == 0
    source = jnp.where(inside, video.reshape(rows, channels), 0).astype(jnp.bfloat16)
    target = jnp.where(inside, cotangent.reshape(rows, channels), 0).astype(jnp.bfloat16)
    active = jax.nn.silu(source.astype(jnp.float32)).astype(jnp.bfloat16)
    padded = halo_block(jnp.where(is_encoder, active, target))
    early = jnp.where(is_encoder, padded, flat(target))
    early, padded = lax.optimization_barrier((early, padded))
    early_all = lax.all_gather(early, "tile", axis=0)
    early_all = lax.all_gather(early_all, "clip", axis=0)
    early_all = early_all.reshape((-1,) + early.shape)
    mixed = conv_dot(padded, kernel, rows, columns, True)
    hidden = jnp.where(inside, source.astype(jnp.float32) + mixed, 0.0).astype(jnp.bfloat16)
    latent = shifted(hidden, "segment", 1)
    wide = latent.astype(jnp.float32)
    own_grad = jnp.where(
        inside, target.astype(jnp.float32) + silu_grad(wide) * mixed, 0.0
    ).astype(jnp.bfloat16)
    returned = shifted(own_grad, "segment", -1)
    padded_two = halo_block(jax.nn.silu(wide).astype(jnp.bfloat16))
    late = jnp.where(is_encoder, flat(returned), padded_two)
    late_all = gather_all(late)
    second = conv_dot(padded_two, kernel, rows, columns, False)
    decoded = jnp.where(inside, wide + second, 0.0).astype(jnp.bfloat16)
    own_out = jnp.where(is_encoder, hidden, decoded).reshape(video.shape[2:])
    acts = jnp.where(is_encoder, early_all, late_all)
    ups = jnp.where(is_encoder, late_all, early_all)[:, :rows]
    summed = own_entries(acts, ups, axes, frame_count, height, columns)
    return (own_out[None, None, None], summed[None])


def solution(mesh):
    in_specs = (
        P("clip", "tile", None, None, None, None),
        P("clip", "tile", None, None, None, None),
        P("segment", None, None, None),
        P("clip", "tile", None),
        P("clip", "tile"),
        P("clip"),
    )
    out_specs = (
        P("segment", "clip", "tile", None, None, None, None),
        P("segment", None, ("clip", "tile")),
    )
    return jax.shard_map(local, mesh=mesh, in_specs=in_specs, out_specs=out_specs, check_vma=False)
```
